768 devices in a mesh: row: 96 (over y_hi, z, core), col: 8 (over y_lo, x).
Axes of the slice: x: 4, y: 8 (y_hi: 4, y_lo: 2; y = y_hi * 2 + y_lo), z: 12, core: 2. Of those that a mesh axis runs over, the one named last changes fastest.
Arguments:
- raw_amps: float32 [24576, 3072], P('row', 'col'), may hold values from -24 to 24
- integrals: float32 [3072, 4096], P('row', 'col'), may hold values from -0.109375 to 0.109375
- occ_energy: float32 [256], replicated, may hold values from -2 to -0.5
- vir_energy: float32 [2048], replicated, may hold values from 0.5 to 3
- occ_pairs: int32 [24576, 2], P('row'), may hold values from 0 to 255
- vir_pairs: int32 [3072, 2], replicated, may hold values from 0 to 2047
- pair_order: int32 [3072], replicated, may hold values from 0 to 3071, each once
Outputs:
- residual: float32 [24576, 4096], P('row', 'col')
The draws below stay inside these ranges and needn't reach their ends.
Inputs may be any that keep to these rules, and one draw needn't show every extreme that they name: `pair_order`: each column index appears exactly once.
All inputs are finite; a program needn't handle non-finite values.
Results may differ from the reference program's by a relative error of at most 0.000068.
Values sent between devices are 32-bit elements; how exact they have to be, the bound alone decides.
A program may use at most 64 MiB of HBM per device.

```python
import jax
import jax.numpy as jnp
from jax import lax

NO = 256
NV = 2048
K = 3072
P_SIZE = 24576
Q = 4096


def set_ends(array, stream_key, least, high):
    dims = array.shape
    index_at = [jax.random.randint(jax.random.fold_in(stream_key, axis), (), 0, dims[axis]) for axis in range(len(dims))]
    array = array.at[tuple(index_at)].set(least)
    longest = dims.index(max(dims))
    index_at[longest] = (index_at[longest] + 1) % dims[longest]
    return array.at[tuple(index_at)].set(high)


def steps_of(own_key, extent, shards, low, largest):
    factor_of = 1.0
    for dim, blocks in shards:
        heights = jax.random.uniform(jax.random.fold_in(jax.random.fold_in(own_key, 6), dim), (blocks,), jnp.float32, low / len(shards), largest / len(shards))
        factor_of = factor_of * jnp.repeat(jnp.exp(heights), extent[dim] // blocks).reshape((-1,) + (1,) * (len(extent) - 1 - dim))
    return factor_of


def noise(key, extent, spread, limit, split=(), kind=jnp.bfloat16):
    gain = steps_of(key, extent, split, -0.22, 0.18) if split else 1.0
    result = jax.random.normal(key, extent, jnp.float32) * spread * gain
    return jnp.minimum(jnp.maximum(result, -limit), limit).astype(kind)


def setup_inputs(seed: int = 0) -> dict:
    arg_keys = jax.random.split(jax.random.key(seed), 8)
    raw_amps = noise(arg_keys[0], (P_SIZE, K), 4.0, 24.0, ((0, 96), (1, 8)), jnp.float32)
    integrals = noise(arg_keys[1], (K, Q), K ** -0.5, 0.109375, ((0, 96), (1, 8)), jnp.float32)
    occ_energy = jnp.clip(jax.random.uniform(arg_keys[2], (NO,), jnp.float32, -2.0, -0.5), -2.0, -0.5)
    vir_energy = jnp.clip(jax.random.uniform(arg_keys[3], (NV,), jnp.float32, 0.5, 3.0), 0.5, 3.0)
    occ_pairs = set_ends(jax.random.randint(arg_keys[4], (P_SIZE, 2), 0, NO), jax.random.fold_in(arg_keys[4], 1), 0, NO - 1).astype(jnp.int32)
    vir_pairs = set_ends(jax.random.randint(arg_keys[5], (K, 2), 0, NV), jax.random.fold_in(arg_keys[5], 1), 0, NV - 1).astype(jnp.int32)
    pair_order = jax.random.permutation(arg_keys[6], K).astype(jnp.int32)
    return {"raw_amps": raw_amps, "integrals": integrals, "occ_energy": occ_energy, "vir_energy": vir_energy, "occ_pairs": occ_pairs, "vir_pairs": vir_pairs, "pair_order": pair_order}


def reference(raw_amps, integrals, occ_energy, vir_energy, occ_pairs, vir_pairs, pair_order):
    occ_sum = occ_energy[occ_pairs[:, 0]] + occ_energy[occ_pairs[:, 1]]
    vir_sum = vir_energy[vir_pairs[:, 0]] + vir_energy[vir_pairs[:, 1]]
    denom = vir_sum[None, :] - occ_sum[:, None]
    scaled = raw_amps / denom
    ordered = jnp.take(scaled, pair_order, axis=1)
    return jnp.dot(ordered, integrals, preferred_element_type=jnp.float32, precision=lax.Precision.HIGHEST)
```

```python
import functools

import jax
import jax.numpy as jnp
from jax import lax
from jax.experimental import pallas as pl
from jax.experimental.pallas import tpu as pltpu
from jax.sharding import PartitionSpec as P

MESH = pl.DeviceIdType.MESH
F32, BF16 = jnp.float32, jnp.bfloat16
NX, NYH, NZ = 4, 4, 12
ROWS, WIDTH, DEPTH, COLS = 256, 384, 32, 512
K = 3072
OFFSETS = (0, NYH - 1, 1, 2)
LAST = ((0, 1), (2, 3))


def kernel(
    raw, integ, occ_e, occ_p, vir_e, vir_p, order, out,
    amps, ints, pick, parts, moved, vir_sum, occ_sum,
    rz, ry, rs, ra, sz, sy, ss, sa, local,
):
    row, col = lax.axis_index("row"), lax.axis_index("col")
    core, z, yh = row % 2, (row // 2) % NZ, row // (2 * NZ)
    x, yl = col % NX, col // NX

    def device(x, yl, yh, z, core):
        return ((yh * NZ + z) * 2 + core, yl * NX + x)

    up, down = device(x, yl, yh, (z + 1) % NZ, core), device(x, yl, yh, (z + NZ - 1) % NZ, core)
    north, south = device(x, yl, (yh + 1) % NYH, z, core), device(x, yl, (yh + NYH - 1) % NYH, z, core)
    east, west = device((x + 1) % NX, yl, yh, z, core), device((x + NX - 1) % NX, yl, yh, z, core)
    partner, sibling = device(x, 1 - yl, yh, z, core), device(x, yl, yh, z, 1 - core)
    along_z = (up, down)

    def slot(z, core, yh):
        return z * 8 + core * 4 + yh

    def send(src, dst, ssem, rsem, to):
        pltpu.make_async_remote_copy(
            src_ref=src, dst_ref=dst, send_sem=ssem, recv_sem=rsem, device_id=to, device_id_type=MESH
        ).start()

    def wait(ref, sem):
        pltpu.make_async_copy(ref, ref, sem).wait()

    barrier = pltpu.get_barrier_semaphore()
    for to in (up, down, north, south, east, west, partner, sibling):
        pl.semaphore_signal(barrier, inc=1, device_id=to, device_id_type=MESH)
    pl.semaphore_wait(barrier, 8)

    own = slot(z, core, yh)
    mine = ints.at[own]
    send(integ, mine, sy.at[0], ry.at[0], north)
    send(integ, mine, sy.at[1], ry.at[1], south)
    send(integ, mine, sz.at[0], rz.at[0, 0, 0], up)
    send(integ, mine, sz.at[1], rz.at[1, 0, 0], down)
    g0, g1 = yl * NX, (1 - yl) * NX
    x_w, x_e, x_o = (x + NX - 1) % NX, (x + 1) % NX, (x + 2) % NX

    def half(block, h):
        return amps.at[block, pl.ds(h * (ROWS // 2), ROWS // 2)]

    for h in range(2):
        src = raw.at[pl.ds(h * (ROWS // 2), ROWS // 2)]
        send(src, half(col, h), sa.at[0], ra.at[0, h], east)
        send(src, half(col, h), sa.at[1], ra.at[1, h], west)
        send(src, half(col, h), sa.at[2], ra.at[2, h], partner)
    keep_b = pltpu.make_async_copy(integ, mine, local.at[0])
    keep_a = pltpu.make_async_copy(raw, amps.at[col], local.at[1])
    keep_b.start()
    keep_a.start()

    lane = lax.broadcasted_iota(jnp.int32, (ROWS, 256), 1)
    energy = jnp.broadcast_to(occ_e[...], (ROWS, 256))
    occ_sum[...] = jnp.sum(
        jnp.where(lane == occ_p[:, 0:1], energy, 0.0), axis=1, keepdims=True
    ) + jnp.sum(jnp.where(lane == occ_p[:, 1:2], energy, 0.0), axis=1, keepdims=True)
    table = vir_e[...]
    hi = table.astype(BF16)
    rest = table - hi.astype(F32)
    mid = rest.astype(BF16)
    low = (rest - mid.astype(F32)).astype(BF16)
    table = jnp.concatenate([hi, mid, low], axis=0)

    def vir_block(b, carry):
        total = jnp.zeros((1, WIDTH), F32)
        for j in range(2):
            index = vir_p[pl.ds(j, 1), pl.ds(pl.multiple_of(b * WIDTH, 128), WIDTH)]
            major = index // 128
            minor = index - major * 128
            hot = jnp.where(lax.broadcasted_iota(jnp.int32, (128, WIDTH), 0) == minor, 1.0, 0.0).astype(BF16)
            found = jnp.dot(table, hot, preferred_element_type=F32)
            found = found[0:16] + found[16:32] + found[32:48]
            total += jnp.sum(
                jnp.where(lax.broadcasted_iota(jnp.int32, (16, WIDTH), 0) == major, found, 0.0), axis=0, keepdims=True
            )
        vir_sum[b] = total
        return carry

    lax.fori_loop(0, 8, vir_block, 0)

    def fill(part):
        def some(i, carry):
            at = pl.multiple_of((part * 12 + i) * 64, 64)
            hot = lax.broadcasted_iota(jnp.int32, (64, K), 0) + at == order[...]
            pick[pl.ds(at, 64), :] = jnp.where(hot, 1.0, 0.0).astype(BF16)
            return carry

        lax.fori_loop(0, 12, some, 0)

    def permute(block, first=False):
        scaled = amps[block] / (vir_sum[block] - occ_sum[...])
        hi = scaled.astype(BF16)
        parts[0:ROWS, :] = hi
        parts[ROWS:, :] = (scaled - hi.astype(F32)).astype(BF16)

        def some(i, carry):
            at = pl.ds(pl.multiple_of(i * 512, 512), 512)
            rows = pl.ds(pl.multiple_of(block * WIDTH, 128), WIDTH)
            new = jnp.dot(parts[...], pick[rows, at], preferred_element_type=F32).astype(BF16)
            moved[:, at] = new if first else moved[:, at] + new
            return carry

        lax.fori_loop(0, 6, some, 0)

    def contract(zs):
        rows = ints[pl.ds(zs * 8, 8)].reshape(256, COLS)
        hi = rows.astype(BF16)
        low = (rows - hi.astype(F32)).astype(BF16)
        at = pl.ds(pl.multiple_of(zs * 256, 256), 256)
        a_hi, a_low = moved[0:ROWS, at], moved[ROWS:, at]
        out[...] += (
            jnp.dot(a_hi, hi, preferred_element_type=F32)
            + jnp.dot(a_low, hi, preferred_element_type=F32)
            + jnp.dot(a_hi, low, preferred_element_type=F32)
        )

    y_slots = [slot(z, core, (yh + off) % NYH) for off in OFFSETS]

    def plane(u):
        for way in range(2):
            send(ints.at[y_slots[u]], ints.at[y_slots[u]], sz.at[way], rz.at[way, 0, u], along_z[way])

    def piece(s, h):
        return ints.at[s, pl.ds(h * 16, 16)]

    wait(ints.at[own], ry.at[0])
    send(piece(y_slots[1], 0), piece(y_slots[1], 0), sy.at[2], ry.at[2], north)
    plane(1)
    wait(ints.at[own], ry.at[1])
    send(piece(y_slots[2], 1), piece(y_slots[2], 1), sy.at[3], ry.at[3], south)
    plane(2)

    def group(z, core):
        return ints.at[pl.ds(slot(z, core, 0), 4)]

    def to_sibling(z_from, index):
        send(group(z_from, core), group(z_from, core), ss, rs.at[index], sibling)

    def hop(t, u):
        for way in range(2):
            if t == 6 and u not in LAST[way]:
                continue
            z_from = (z + (NZ - t, t)[way]) % NZ
            s = slot(z_from, core, (yh + OFFSETS[u]) % NYH)
            wait(ints.at[s], rz.at[way, t - 1, u])
            if t < 5 or t == 5 and u in LAST[way]:
                send(ints.at[s], ints.at[s], sz.at[way], rz.at[way, t, u], along_z[way])
            if u == 3 and t < 6:
                to_sibling(z_from, 2 * t - 1 + way)

    def amps_in(index, block, h, then=()):
        wait(half(block, h), ra.at[index, h])
        for way, to_index in then:
            send(half(block, h), half(block, h), sa.at[way], ra.at[to_index, h], (east, west)[way])

    fill(0)
    wait(piece(own, 0), ry.at[2])
    wait(piece(own, 1), ry.at[3])
    plane(3)
    keep_b.wait()
    to_sibling(z, 0)
    keep_a.wait()
    hop(1, 0)
    fill(1)
    hop(1, 1)
    amps_in(0, g0 + x_w, 0, [(0, 3)])
    amps_in(2, g1 + x, 0, [(0, 4), (1, 5)])
    fill(2)
    hop(1, 2)
    fill(3)
    hop(1, 3)
    hop(2, 0)
    permute(col, True)
    hop(2, 1)
    amps_in(0, g0 + x_w, 1, [(0, 3)])
    amps_in(2, g1 + x, 1, [(0, 4), (1, 5)])
    hop(2, 2)
    permute(g0 + x_w)
    hop(2, 3)
    hop(3, 0)
    amps_in(1, g0 + x_e, 0)
    amps_in(1, g0 + x_e, 1)
    permute(g0 + x_e)
    hop(3, 1)
    amps_in(5, g1 + x_e, 0, [(1, 6)])
    hop(3, 2)
    permute(g1 + x)
    hop(3, 3)
    hop(4, 0)
    amps_in(5, g1 + x_e, 1, [(1, 6)])
    hop(4, 1)
    permute(g1 + x_e)
    hop(4, 2)
    amps_in(3, g0 + x_o, 0)
    amps_in(3, g0 + x_o, 1)
    permute(g0 + x_o)
    hop(4, 3)
    hop(5, 0)
    hop(5, 1)
    amps_in(4, g1 + x_w, 0)
    hop(5, 2)
    hop(5, 3)
    amps_in(4, g1 + x_w, 1)
    permute(g1 + x_w)
    for h in range(2):
        amps_in(6, g1 + x_o, h)
    permute(g1 + x_o)
    for i in range(11):
        wait(group(z, 0), rs.at[i])
    out[...] = jnp.zeros_like(out)

    def near(i, carry):
        contract((z + 7 + i) % NZ)
        return carry

    lax.fori_loop(0, 11, near, 0)
    for u in range(4):
        hop(6, u)
    z_far = (z + 6) % NZ
    to_sibling(z_far, 11)
    wait(group(z, 0), rs.at[11])
    contract(z_far)

    for way in range(2):
        wait(ints.at[pl.ds(0, 22)], sz.at[way])
        wait(ints.at[0], sy.at[way])
        wait(piece(0, 0), sy.at[2 + way])
        wait(amps.at[pl.ds(0, 3)], sa.at[way])
    wait(amps.at[0], sa.at[2])
    wait(ints.at[pl.ds(0, 48)], ss)


def on_device(raw_amps, integrals, occ_energy, vir_energy, occ_pairs, vir_pairs, pair_order):
    order = pair_order.reshape(NYH, NZ, 2, DEPTH).transpose(1, 2, 0, 3).reshape(1, K)
    vmem = pl.BlockSpec(memory_space=pltpu.VMEM)
    hbm = pl.BlockSpec(memory_space=pl.ANY)
    dma = pltpu.SemaphoreType.DMA
    return pl.pallas_call(
        kernel,
        out_shape=jax.ShapeDtypeStruct((ROWS, COLS), F32),
        in_specs=[hbm, hbm] + [vmem] * 5,
        out_specs=vmem,
        scratch_shapes=[
            pltpu.VMEM((8, ROWS, WIDTH), F32),
            pltpu.VMEM((96, DEPTH, COLS), F32),
            pltpu.VMEM((K, K), BF16),
            pltpu.VMEM((2 * ROWS, WIDTH), BF16),
            pltpu.VMEM((2 * ROWS, K), BF16),
            pltpu.VMEM((8, 1, WIDTH), F32),
            pltpu.VMEM((ROWS, 1), F32),
            dma((2, 6, 4)),
            dma((4,)),
            dma((12,)),
            dma((7, 2)),
            dma((2,)),
            dma((4,)),
            dma(()),
            dma((3,)),
            dma((2,)),
        ],
        compiler_params=pltpu.CompilerParams(
            collective_id=0, has_side_effects=True, vmem_limit_bytes=56 << 20
        ),
    )(
        raw_amps,
        integrals,
        occ_energy.reshape(1, 256),
        occ_pairs,
        vir_energy.reshape(16, 128),
        vir_pairs.T,
        order,
    )


def solution(mesh):
    placed = (P("row", "col"), P("row", "col"), P(), P(), P("row", None), P(), P())
    return jax.shard_map(
        on_device, mesh=mesh, in_specs=placed, out_specs=P("row", "col"), check_vma=False
    )
```

```python
import functools

import jax
import jax.numpy as jnp
from jax import lax
from jax.experimental import pallas as pl
from jax.experimental.pallas import tpu as pltpu
from jax.sharding import PartitionSpec as P

MESH = pl.DeviceIdType.MESH
F32, BF16 = jnp.float32, jnp.bfloat16
NX, NYH, NZ = 4, 4, 12
ROWS, WIDTH, DEPTH, COLS = 256, 384, 32, 512
K = 3072
OFFSETS = (0, NYH - 1, 1, 2)
def kernel(
    raw, integ, occ_e, occ_p, vir_e, vir_p, order, out,
    amps, ints, pick, parts, moved, vir_sum, occ_sum, turned, place,
    rz, ry, rs, ra, rf, sz, sy, ss, sa, sf, local,
):
    row, col = lax.axis_index("row"), lax.axis_index("col")
    core, z, yh = row % 2, (row // 2) % NZ, row // (2 * NZ)
    x, yl = col % NX, col // NX

    def device(x, yl, yh, z, core):
        return ((yh * NZ + z) * 2 + core, yl * NX + x)

    up, down = device(x, yl, yh, (z + 1) % NZ, core), device(x, yl, yh, (z + NZ - 1) % NZ, core)
    north, south = device(x, yl, (yh + 1) % NYH, z, core), device(x, yl, (yh + NYH - 1) % NYH, z, core)
    east, west = device((x + 1) % NX, yl, yh, z, core), device((x + NX - 1) % NX, yl, yh, z, core)
    partner, sibling = device(x, 1 - yl, yh, z, core), device(x, yl, yh, z, 1 - core)
    along_z = (up, down)

    def slot(z, core, yh):
        return z * 8 + core * 4 + yh

    def send(src, dst, ssem, rsem, to):
        pltpu.make_async_remote_copy(
            src_ref=src, dst_ref=dst, send_sem=ssem, recv_sem=rsem, device_id=to, device_id_type=MESH
        ).start()

    def wait(ref, sem):
        pltpu.make_async_copy(ref, ref, sem).wait()

    barrier = pltpu.get_barrier_semaphore()
    for to in (up, down, north, south, east, west, partner, sibling):
        pl.semaphore_signal(barrier, inc=1, device_id=to, device_id_type=MESH)
    pl.semaphore_wait(barrier, 8)

    own = slot(z, core, yh)
    mine = ints.at[own]
    send(integ, mine, sy.at[0], ry.at[0], north)
    send(integ, mine, sy.at[1], ry.at[1], south)
    send(integ, mine, sz.at[0], rz.at[0, 0, 0], up)
    send(integ, mine, sz.at[1], rz.at[1, 0, 0], down)
    g0, g1 = yl * NX, (1 - yl) * NX
    x_w, x_e, x_o = (x + NX - 1) % NX, (x + 1) % NX, (x + 2) % NX

    def half(block, h):
        return amps.at[block, pl.ds(h * (ROWS // 2), ROWS // 2)]

    for h in range(2):
        for way, to in ((0, east), (1, west)):
            g = (h, 1 - h)[way]
            send(raw.at[pl.ds(g * (ROWS // 2), ROWS // 2)], half(col, g), sa.at[way], ra.at[way, g], to)
    keep_b = pltpu.make_async_copy(integ, mine, local.at[0])
    keep_a = pltpu.make_async_copy(raw, amps.at[col], local.at[1])
    keep_b.start()
    keep_a.start()

    sub = lax.broadcasted_iota(jnp.int32, (ROWS, 256), 0)
    lane = lax.broadcasted_iota(jnp.int32, (ROWS, 256), 1)
    energy = jnp.broadcast_to(occ_e[...], (ROWS, 256))
    total = jnp.zeros((ROWS, 1), F32)
    for j in range(2):
        orbital = jnp.broadcast_to(occ_p[j : j + 1, :].astype(F32), (ROWS, 256))
        orbital = jnp.sum(jnp.where(sub == lane, orbital, 0.0), axis=1, keepdims=True)
        total += jnp.sum(jnp.where(lane.astype(F32) == orbital, energy, 0.0), axis=1, keepdims=True)
    occ_sum[...] = total

    for shift in range(4):
        turned[shift] = order[...] if shift == 0 else pltpu.roll(order[...], shift * 32, 1)
    quarter = lax.broadcasted_iota(jnp.int32, (1, 128), 1) // 32
    for zs in range(NZ):
        for c in range(2):
            found = None
            for ys in range(NYH):
                here = turned[(ys - zs % 2 * 2 - c) % 4, pl.ds(ys * 6 + zs // 2, 1), :]
                found = here if found is None else jnp.where(quarter == ys, here, found)
            place[:, pl.ds(zs * 256 + c * 128, 128)] = found

    table = vir_e[...]
    hi = table.astype(BF16)
    rest = table - hi.astype(F32)
    mid = rest.astype(BF16)
    low = (rest - mid.astype(F32)).astype(BF16)
    table = jnp.concatenate([hi, mid, low], axis=0)

    def vir_block(b, carry):
        total = jnp.zeros((1, WIDTH), F32)
        for j in range(2):
            index = vir_p[pl.ds(j, 1), pl.ds(pl.multiple_of(b * WIDTH, 128), WIDTH)]
            major = index // 128
            minor = index - major * 128
            hot = jnp.where(lax.broadcasted_iota(jnp.int32, (128, WIDTH), 0) == minor, 1.0, 0.0).astype(BF16)
            found = jnp.dot(table, hot, preferred_element_type=F32)
            found = found[0:16] + found[16:32] + found[32:48]
            total += jnp.sum(
                jnp.where(lax.broadcasted_iota(jnp.int32, (16, WIDTH), 0) == major, found, 0.0), axis=0, keepdims=True
            )
        vir_sum[b] = total
        return carry

    blocks = [col, g0 + x_w, g0 + x_e, g1 + x, g0 + x_o, g1 + x_e, g1 + x_w, g1 + x_o]

    def fill(p):
        def some(i, carry):
            hot = lax.broadcasted_iota(jnp.int32, (64, K), 0) + (blocks[p] * WIDTH + i * 64) == place[...]
            pick[pl.ds(pl.multiple_of(p * WIDTH + i * 64, 64), 64), :] = jnp.where(hot, 1.0, 0.0).astype(BF16)
            return carry

        lax.fori_loop(0, 6, some, 0)

    def scale(p):
        scaled = amps[blocks[p]] / (vir_sum[blocks[p]] - occ_sum[...])
        hi = scaled.astype(BF16)
        parts[0:ROWS, p * WIDTH : (p + 1) * WIDTH] = hi
        parts[ROWS:, p * WIDTH : (p + 1) * WIDTH] = (scaled - hi.astype(F32)).astype(BF16)

    def permute(p, count, events=()):
        def some(i, carry):
            at = pl.ds(pl.multiple_of(i * 1024, 1024), 1024)
            here = slice(p * WIDTH, (p + count) * WIDTH)
            new = jnp.dot(parts[:, here], pick[here, at], preferred_element_type=F32).astype(BF16)
            moved[:, at] = new if p == 0 else moved[:, at] + new
            for j, event in enumerate(events):
                pl.when(i == j)(event)
            return carry

        lax.fori_loop(0, 3, some, 0)

    def contract(zs):
        rows = ints[pl.ds(zs * 8, 8)].reshape(256, COLS)
        hi = rows.astype(BF16)
        low = (rows - hi.astype(F32)).astype(BF16)
        at = pl.ds(pl.multiple_of(zs * 256, 256), 256)
        a_hi, a_low = moved[0:ROWS, at], moved[ROWS:, at]
        out[...] += (
            jnp.dot(a_hi, hi, preferred_element_type=F32)
            + jnp.dot(a_low, hi, preferred_element_type=F32)
            + jnp.dot(a_hi, low, preferred_element_type=F32)
        )

    y_slots = [slot(z, core, (yh + off) % NYH) for off in OFFSETS]

    def plane(u):
        for way in range(2):
            send(ints.at[y_slots[u]], ints.at[y_slots[u]], sz.at[way], rz.at[way, 0, u], along_z[way])

    def piece(s, h):
        return ints.at[s, pl.ds(h * 16, 16)]

    def group(z, core):
        return ints.at[pl.ds(slot(z, core, 0), 4)]

    def to_sibling(z_from, index):
        send(group(z_from, core), group(z_from, core), ss, rs.at[index], sibling)

    def source(t, way):
        return (z + (NZ - t, t)[way]) % NZ

    def hop(t, u):
        for way in range(2):
            s = slot(source(t, way), core, (yh + OFFSETS[u]) % NYH)
            wait(ints.at[s], rz.at[way, t - 1, u])
            if t < 5:
                send(ints.at[s], ints.at[s], sz.at[way], rz.at[way, t, u], along_z[way])
            elif u == 0:
                send(piece(s, way), piece(s, way), sz.at[way], rz.at[way, 5, 0], along_z[way])
            if u == 3:
                to_sibling(source(t, way), 2 * t - 1 + way)

    def hops(*pairs):
        def event():
            for t, u in pairs:
                hop(t, u)

        return event

    def amps_in(index, p, h, then=()):
        block = blocks[p]
        wait(half(block, h), ra.at[index, h])
        for way, to_index in then:
            send(half(block, h), half(block, h), sa.at[way], ra.at[to_index, h], (east, west)[way])

    z_far = (z + 6) % NZ
    f_slots = [slot(z_far, core, (yh + off) % NYH) for off in OFFSETS]

    def far_in():
        for way in range(2):
            here = piece(f_slots[0], way)
            wait(here, rz.at[way, 5, 0])
            send(here, here, sf.at[0], rf.at[0, way], north)
            send(here, here, sf.at[1], rf.at[1, way], south)

    def far_on():
        for way in range(2):
            here = piece(f_slots[1 + way], way)
            wait(here, rf.at[way, way])
            send(here, here, sf.at[way], rf.at[2, way], (north, south)[way])

    def far_end():
        for way in range(2):
            wait(piece(f_slots[1 + way], 1 - way), rf.at[way, 1 - way])
            wait(piece(f_slots[3], way), rf.at[2, way])

    fill(0)
    fill(1)
    hop(1, 0)
    wait(ints.at[own], ry.at[0])
    send(piece(y_slots[1], 0), piece(y_slots[1], 0), sy.at[2], ry.at[2], north)
    plane(1)
    wait(ints.at[own], ry.at[1])
    send(piece(y_slots[2], 1), piece(y_slots[2], 1), sy.at[3], ry.at[3], south)
    plane(2)
    for h in range(2):
        send(raw.at[pl.ds(h * (ROWS // 2), ROWS // 2)], half(col, h), sa.at[2], ra.at[2, h], partner)
    lax.fori_loop(0, 8, vir_block, 0)
    amps_in(0, 1, 0, [(0, 3)])
    amps_in(1, 2, 1, [(1, 3)])
    hop(2, 0)
    wait(piece(own, 0), ry.at[2])
    wait(piece(own, 1), ry.at[3])
    plane(3)
    keep_b.wait()
    to_sibling(z, 0)
    fill(2)
    fill(3)
    hop(1, 1)
    keep_a.wait()
    scale(0)
    fill(4)
    hop(1, 2)

    def partner_in(h):
        amps_in(2, 3, h, [(0, 4), (1, 5)])

    permute(0, 1, [hops((3, 0)), hops((1, 3)), hops((2, 1))])
    partner_in(0)
    amps_in(0, 1, 1)
    amps_in(1, 2, 0)
    scale(1)
    scale(2)
    permute(1, 2, [hops((2, 2)), hops((4, 0)), hops((2, 3))])
    partner_in(1)
    fill(5)
    hop(3, 1)
    amps_in(3, 4, 0)
    amps_in(3, 4, 1)
    scale(3)
    scale(4)
    hop(3, 2)
    amps_in(4, 6, 0, [(0, 6)])
    permute(3, 2, [hops((5, 0)), hops((3, 3)), hops((4, 1))])
    amps_in(5, 5, 1, [(1, 6)])
    fill(6)
    hop(4, 2)
    fill(7)
    amps_in(4, 6, 1)
    amps_in(5, 5, 0)
    scale(5)
    scale(6)
    far_in()
    permute(5, 2, [hops((4, 3)), hops((5, 1))])
    far_on()
    for h in range(2):
        amps_in(6, 7, h)
    scale(7)
    permute(7, 1)
    hop(5, 2)
    hop(5, 3)
    for i in range(9):
        wait(group(z, 0), rs.at[i])
    out[...] = jnp.zeros_like(out)

    def near(i, carry):
        contract((z + 8 + i) % NZ)
        return carry

    lax.fori_loop(0, 9, near, 0)
    far_end()
    to_sibling(z_far, 11)
    for i in range(9, 11):
        wait(group(z, 0), rs.at[i])
    contract((z + 5) % NZ)
    contract((z + 7) % NZ)
    wait(group(z, 0), rs.at[11])
    contract(z_far)

    for way in range(2):
        wait(ints.at[pl.ds(0, 41), pl.ds(0, 16)], sz.at[way])
        wait(ints.at[0], sy.at[way])
        wait(piece(0, 0), sy.at[2 + way])
        wait(ints.at[pl.ds(0, 3), pl.ds(0, 16)], sf.at[way])
        wait(amps.at[pl.ds(0, 3)], sa.at[way])
    wait(amps.at[0], sa.at[2])
    wait(ints.at[pl.ds(0, 48)], ss)


def on_device(raw_amps, integrals, occ_energy, vir_energy, occ_pairs, vir_pairs, pair_order):
    vmem = pl.BlockSpec(memory_space=pltpu.VMEM)
    hbm = pl.BlockSpec(memory_space=pl.ANY)
    dma = pltpu.SemaphoreType.DMA
    return pl.pallas_call(
        kernel,
        out_shape=pltpu.VMEM((ROWS, COLS), F32),
        in_specs=[hbm, hbm] + [vmem] * 5,
        out_specs=vmem,
        scratch_shapes=[
            pltpu.VMEM((8, ROWS, WIDTH), F32),
            pltpu.VMEM((96, DEPTH, COLS), F32),
            pltpu.VMEM((K, K), BF16),
            pltpu.VMEM((2 * ROWS, K), BF16),
            pltpu.VMEM((2 * ROWS, K), BF16),
            pltpu.VMEM((8, 1, WIDTH), F32),
            pltpu.VMEM((ROWS, 1), F32),
            pltpu.VMEM((4, 24, 128), jnp.int32),
            pltpu.VMEM((1, K), jnp.int32),
            dma((2, 6, 4)),
            dma((4,)),
            dma((12,)),
            dma((7, 2)),
            dma((3, 2)),
            dma((2,)),
            dma((4,)),
            dma(()),
            dma((3,)),
            dma((2,)),
            dma((2,)),
        ],
        compiler_params=pltpu.CompilerParams(
            collective_id=0, has_side_effects=True, vmem_limit_bytes=56 << 20
        ),
    )(
        raw_amps,
        integrals,
        occ_energy.reshape(1, 256),
        occ_pairs.T,
        vir_energy.reshape(16, 128),
        vir_pairs.T,
        pair_order.reshape(24, 128),
    )


def solution(mesh):
    placed = (P("row", "col"), P("row", "col"), P(), P(), P("row", None), P(), P())
    return jax.shard_map(
        on_device, mesh=mesh, in_specs=placed, out_specs=P("row", "col"), check_vma=False
    )
```

```python
import functools

import jax
import jax.numpy as jnp
from jax import lax
from jax.experimental import pallas as pl
from jax.experimental.pallas import tpu as pltpu
from jax.sharding import PartitionSpec as P

MESH = pl.DeviceIdType.MESH
F32, BF16 = jnp.float32, jnp.bfloat16
NX, NYH, NZ = 4, 4, 12
ROWS, WIDTH, DEPTH, COLS = 256, 384, 32, 512
K = 3072
OFFSETS = (0, NYH - 1, 1, 2)
def kernel(
    raw, integ, occ_e, occ_p, vir_e, vir_p, order, out,
    amps, ints, pick, parts, moved, vir_sum, occ_sum, turned, place,
    rz, ry, rs, ra, rb, rf, sz, sy, ss, sa, sf, local,
):
    row, col = lax.axis_index("row"), lax.axis_index("col")
    core, z, yh = row % 2, (row // 2) % NZ, row // (2 * NZ)
    x, yl = col % NX, col // NX

    def device(x, yl, yh, z, core):
        return ((yh * NZ + z) * 2 + core, yl * NX + x)

    up, down = device(x, yl, yh, (z + 1) % NZ, core), device(x, yl, yh, (z + NZ - 1) % NZ, core)
    north, south = device(x, yl, (yh + 1) % NYH, z, core), device(x, yl, (yh + NYH - 1) % NYH, z, core)
    east, west = device((x + 1) % NX, yl, yh, z, core), device((x + NX - 1) % NX, yl, yh, z, core)
    up2, down2 = device(x, yl, yh, (z + 2) % NZ, core), device(x, yl, yh, (z + NZ - 2) % NZ, core)
    partner, sibling = device(x, 1 - yl, yh, z, core), device(x, yl, yh, z, 1 - core)
    along_z = (up, down)

    def slot(z, core, yh):
        return z * 8 + core * 4 + yh

    def send(src, dst, ssem, rsem, to):
        pltpu.make_async_remote_copy(
            src_ref=src, dst_ref=dst, send_sem=ssem, recv_sem=rsem, device_id=to, device_id_type=MESH
        ).start()

    def wait(ref, sem):
        pltpu.make_async_copy(ref, ref, sem).wait()

    barrier = pltpu.get_barrier_semaphore()
    for to in (up, down, up2, down2, north, south, east, west, partner, sibling):
        pl.semaphore_signal(barrier, inc=1, device_id=to, device_id_type=MESH)
    pl.semaphore_wait(barrier, 10)

    own = slot(z, core, yh)
    mine = ints.at[own]
    for h in range(2):
        for way, to in ((0, north), (1, south)):
            g = (h, 1 - h)[way]
            send(integ.at[pl.ds(g * 16, 16)], ints.at[own, pl.ds(g * 16, 16)], sy.at[way], ry.at[way, g], to)
    send(integ, mine, sz.at[0], rz.at[0, 0, 0], up)
    send(integ, mine, sz.at[1], rz.at[1, 0, 0], down)
    send(integ, mine, sz.at[0], rz.at[0, 1, 0], up2)
    send(integ, mine, sz.at[1], rz.at[1, 1, 0], down2)
    g0, g1 = yl * NX, (1 - yl) * NX
    x_w, x_e, x_o = (x + NX - 1) % NX, (x + 1) % NX, (x + 2) % NX

    def half(block, h):
        return amps.at[block, pl.ds(h * (ROWS // 2), ROWS // 2)]

    for h in range(2):
        for way, to in ((0, east), (1, west)):
            send(raw.at[pl.ds(h * (ROWS // 2), ROWS // 2)], half(col, h), sa.at[way], ra.at[way, h], to)
    keep_b = pltpu.make_async_copy(integ, mine, local.at[0])
    keep_a = pltpu.make_async_copy(raw, amps.at[col], local.at[1])
    keep_b.start()
    keep_a.start()

    sub = lax.broadcasted_iota(jnp.int32, (ROWS, 256), 0)
    lane = lax.broadcasted_iota(jnp.int32, (ROWS, 256), 1)
    energy = jnp.broadcast_to(occ_e[...], (ROWS, 256))
    total = jnp.zeros((ROWS, 1), F32)
    for j in range(2):
        orbital = jnp.broadcast_to(occ_p[j : j + 1, :].astype(F32), (ROWS, 256))
        orbital = jnp.sum(jnp.where(sub == lane, orbital, 0.0), axis=1, keepdims=True)
        total += jnp.sum(jnp.where(lane.astype(F32) == orbital, energy, 0.0), axis=1, keepdims=True)
    occ_sum[...] = total

    for shift in range(4):
        turned[shift] = order[...] if shift == 0 else pltpu.roll(order[...], shift * 32, 1)
    quarter = lax.broadcasted_iota(jnp.int32, (1, 128), 1) // 32
    for zs in range(NZ):
        for c in range(2):
            found = None
            for ys in range(NYH):
                here = turned[(ys - zs % 2 * 2 - c) % 4, pl.ds(ys * 6 + zs // 2, 1), :]
                found = here if found is None else jnp.where(quarter == ys, here, found)
            place[:, pl.ds(zs * 256 + c * 128, 128)] = found

    table = vir_e[...]
    hi = table.astype(BF16)
    rest = table - hi.astype(F32)
    mid = rest.astype(BF16)
    low = (rest - mid.astype(F32)).astype(BF16)
    table = jnp.concatenate([hi, mid, low], axis=0)

    def vir_block(b, carry):
        total = jnp.zeros((1, WIDTH), F32)
        for j in range(2):
            index = vir_p[pl.ds(j, 1), pl.ds(pl.multiple_of(b * WIDTH, 128), WIDTH)]
            major = index // 128
            minor = index - major * 128
            hot = jnp.where(lax.broadcasted_iota(jnp.int32, (128, WIDTH), 0) == minor, 1.0, 0.0).astype(BF16)
            found = jnp.dot(table, hot, preferred_element_type=F32)
            found = found[0:16] + found[16:32] + found[32:48]
            total += jnp.sum(
                jnp.where(lax.broadcasted_iota(jnp.int32, (16, WIDTH), 0) == major, found, 0.0), axis=0, keepdims=True
            )
        vir_sum[b] = total
        return carry

    blocks = [col, g0 + x_w, g0 + x_e, g1 + x, g0 + x_o, g1 + x_e, g1 + x_w, g1 + x_o]

    def fill(p):
        def some(i, carry):
            hot = lax.broadcasted_iota(jnp.int32, (64, K), 0) + (blocks[p] * WIDTH + i * 64) == place[...]
            pick[pl.ds(pl.multiple_of(p * WIDTH + i * 64, 64), 64), :] = jnp.where(hot, 1.0, 0.0).astype(BF16)
            return carry

        lax.fori_loop(0, 6, some, 0)

    def scale(p):
        scaled = amps[blocks[p]] / (vir_sum[blocks[p]] - occ_sum[...])
        hi = scaled.astype(BF16)
        parts[0:ROWS, p * WIDTH : (p + 1) * WIDTH] = hi
        parts[ROWS:, p * WIDTH : (p + 1) * WIDTH] = (scaled - hi.astype(F32)).astype(BF16)

    def permute(p, count, events=()):
        def some(i, carry):
            at = pl.ds(pl.multiple_of(i * 1024, 1024), 1024)
            here = slice(p * WIDTH, (p + count) * WIDTH)
            new = jnp.dot(parts[:, here], pick[here, at], preferred_element_type=F32).astype(BF16)
            moved[:, at] = new if p == 0 else moved[:, at] + new
            for j, event in enumerate(events):
                pl.when(i == j)(event)
            return carry

        lax.fori_loop(0, 3, some, 0)

    def contract(chosen):
        rows = jnp.concatenate(
            [ints[pl.ds(z_from * 8 + first, n)].reshape(n * DEPTH, COLS) for z_from, first, n in chosen], axis=0
        )
        hi = rows.astype(BF16)
        low = (rows - hi.astype(F32)).astype(BF16)
        at = [
            pl.ds(pl.multiple_of(z_from * 256 + first * DEPTH, 128), n * DEPTH) for z_from, first, n in chosen
        ]
        a_hi = jnp.concatenate([moved[0:ROWS, cols] for cols in at], axis=1)
        a_low = jnp.concatenate([moved[ROWS:, cols] for cols in at], axis=1)
        out[...] += (
            jnp.dot(a_hi, hi, preferred_element_type=F32)
            + jnp.dot(a_low, hi, preferred_element_type=F32)
            + jnp.dot(a_hi, low, preferred_element_type=F32)
        )

    y_slots = [slot(z, core, (yh + off) % NYH) for off in OFFSETS]

    def plane(u, h):
        here = piece(y_slots[u], h)
        for way in range(2):
            send(here, here, sz.at[way], rz.at[way, 0, u], along_z[way])

    def piece(s, h):
        return ints.at[s, pl.ds(h * 16, 16)]

    def group(z, core):
        return ints.at[pl.ds(slot(z, core, 0), 4)]

    def to_sibling(z_from, index):
        send(group(z_from, core), group(z_from, core), ss, rs.at[index], sibling)

    def source(t, way):
        return (z + (NZ - t, t)[way]) % NZ

    def block_to_sibling(s, index):
        send(ints.at[s], ints.at[s], ss, rs.at[index], sibling)

    def hop(t, u):
        for way in range(2):
            s = slot(source(t, way), core, (yh + OFFSETS[u]) % NYH)
            wait(ints.at[s], rz.at[way, t - 1, u])
            if t < 5 and (t, u) != (1, 0):
                send(ints.at[s], ints.at[s], sz.at[way], rz.at[way, t, u], along_z[way])
            elif t == 5 and u == 0:
                send(piece(s, way), piece(s, way), sz.at[way], rz.at[way, 5, 0], along_z[way])
            if t == 5:
                block_to_sibling(s, 9 + way)
            elif u == 3:
                to_sibling(source(t, way), 2 * t - 1 + way)

    def quarter_of(block, h, way):
        return amps.at[block, pl.ds(h * (ROWS // 2) + way * (ROWS // 4), ROWS // 4)]

    def amps_in(far, h):
        for way, p in ((0, (1, 6)[far]), (1, (2, 5)[far])):
            wait(half(blocks[p], h), ra.at[(0, 3)[far] + way, h])
            here = quarter_of(blocks[p], h, way)
            send(here, here, sa.at[way], rb.at[far, h, way], (east, west)[way])

    def partner_in(h):
        wait(half(blocks[3], h), ra.at[2, h])
        for way in range(2):
            here = half(blocks[3], h)
            send(here, here, sa.at[way], ra.at[3 + way, h], (east, west)[way])

    def opposite_in(far):
        for h in range(2):
            for way in range(2):
                wait(quarter_of(blocks[(4, 7)[far]], h, way), rb.at[far, h, way])

    z_far = (z + 6) % NZ
    f_slots = [slot(z_far, core, (yh + off) % NYH) for off in OFFSETS]

    def far_in():
        for way in range(2):
            here = piece(f_slots[0], way)
            wait(here, rz.at[way, 5, 0])
            send(here, here, sf.at[0], rf.at[0, way], north)
            send(here, here, sf.at[1], rf.at[1, way], south)

    def far_on():
        for way in range(2):
            here = piece(f_slots[1 + way], way)
            wait(here, rf.at[way, way])
            send(here, here, sf.at[way], rf.at[2, way], (north, south)[way])

    def far_end():
        for way in range(2):
            wait(piece(f_slots[1 + way], 1 - way), rf.at[way, 1 - way])
            wait(piece(f_slots[3], way), rf.at[2, way])
        to_sibling(z_far, 11)

    def side_in(h, way):
        wait(piece(y_slots[1 + way], h), ry.at[way, h])
        if h == way:
            send(piece(y_slots[1 + way], h), piece(y_slots[1 + way], h), sy.at[2 + way], ry.at[2, way], (north, south)[way])
        plane(1 + way, h)

    def steps(*calls):
        def event():
            for call, *args in calls:
                call(*args)

        return event

    def plane_end():
        for h in range(2):
            wait(piece(y_slots[3], h), ry.at[2, h])
            plane(3, h)
        keep_b.wait()
        to_sibling(z, 0)

    lax.fori_loop(0, 8, vir_block, 0)
    fill(0)
    fill(1)
    keep_a.wait()
    scale(0)
    side_in(0, 0)
    side_in(1, 1)
    fill(2)
    side_in(1, 0)
    side_in(0, 1)
    for h in range(2):
        send(raw.at[pl.ds(h * (ROWS // 2), ROWS // 2)], half(col, h), sa.at[2], ra.at[2, h], partner)
    hop(1, 0)
    hop(2, 0)
    permute(0, 1, [steps((amps_in, 0, 0)), steps((plane_end,))])
    fill(3)
    hop(1, 1)
    fill(4)
    amps_in(0, 1)
    hop(3, 0)
    scale(1)
    scale(2)
    hop(1, 2)
    hop(1, 3)
    partner_in(0)
    permute(1, 2, [steps((hop, 2, 1)), steps((hop, 4, 0)), steps((hop, 2, 2))])
    partner_in(1)
    fill(5)
    hop(2, 3)
    opposite_in(0)
    scale(3)
    scale(4)
    hop(5, 0)
    hop(3, 1)
    amps_in(1, 0)
    permute(3, 2, [steps((hop, 3, 2)), steps((far_in,), (hop, 3, 3)), steps((amps_in, 1, 1))])
    scale(5)
    scale(6)
    hop(4, 1)
    fill(6)
    fill(7)
    permute(5, 2, [steps((hop, 4, 2)), steps((hop, 4, 3)), steps((far_on,))])
    opposite_in(1)
    scale(7)
    permute(7, 1, [steps((hop, 5, 1)), steps((hop, 5, 2)), steps((hop, 5, 3))])
    for i in range(9):
        wait(group(z, 0), rs.at[i])
    out[...] = jnp.zeros_like(out)

    def near(i, carry):
        contract([((z + 8 + i * 3 + j) % NZ, 0, 8) for j in range(3)])
        pl.when(i == 0)(far_end)
        return carry

    lax.fori_loop(0, 3, near, 0)
    contract([(z_from, core * 4, 4) for z_from in ((z + 5) % NZ, z_far, (z + 7) % NZ)])
    for i in range(9, 12):
        wait(group(z, 0), rs.at[i])
    contract([(z_from, 4 - core * 4, 4) for z_from in ((z + 5) % NZ, z_far, (z + 7) % NZ)])

    for way in range(2):
        wait(ints.at[pl.ds(0, 41), pl.ds(0, 16)], sz.at[way])
        wait(ints.at[0], sy.at[way])
        wait(piece(0, 0), sy.at[2 + way])
        wait(ints.at[pl.ds(0, 3), pl.ds(0, 16)], sf.at[way])
        wait(amps.at[pl.ds(0, 3)], sa.at[way])
    wait(amps.at[0], sa.at[2])
    wait(ints.at[pl.ds(0, 48)], ss)


def on_device(raw_amps, integrals, occ_energy, vir_energy, occ_pairs, vir_pairs, pair_order):
    vmem = pl.BlockSpec(memory_space=pltpu.VMEM)
    hbm = pl.BlockSpec(memory_space=pl.ANY)
    dma = pltpu.SemaphoreType.DMA
    return pl.pallas_call(
        kernel,
        out_shape=pltpu.VMEM((ROWS, COLS), F32),
        in_specs=[hbm, hbm] + [vmem] * 5,
        out_specs=vmem,
        scratch_shapes=[
            pltpu.VMEM((8, ROWS, WIDTH), F32),
            pltpu.VMEM((96, DEPTH, COLS), F32),
            pltpu.VMEM((K, K), BF16),
            pltpu.VMEM((2 * ROWS, K), BF16),
            pltpu.VMEM((2 * ROWS, K), BF16),
            pltpu.VMEM((8, 1, WIDTH), F32),
            pltpu.VMEM((ROWS, 1), F32),
            pltpu.VMEM((4, 24, 128), jnp.int32),
            pltpu.VMEM((1, K), jnp.int32),
            dma((2, 6, 4)),
            dma((3, 2)),
            dma((12,)),
            dma((5, 2)),
            dma((2, 2, 2)),
            dma((3, 2)),
            dma((2,)),
            dma((4,)),
            dma(()),
            dma((3,)),
            dma((2,)),
            dma((2,)),
        ],
        compiler_params=pltpu.CompilerParams(
            collective_id=0, has_side_effects=True, vmem_limit_bytes=56 << 20
        ),
    )(
        raw_amps,
        integrals,
        occ_energy.reshape(1, 256),
        occ_pairs.T,
        vir_energy.reshape(16, 128),
        vir_pairs.T,
        pair_order.reshape(24, 128),
    )


def solution(mesh):
    placed = (P("row", "col"), P("row", "col"), P(), P(), P("row", None), P(), P())
    return jax.shard_map(
        on_device, mesh=mesh, in_specs=placed, out_specs=P("row", "col"), check_vma=False
    )
```

```python
import functools

import jax
import jax.numpy as jnp
from jax import lax
from jax.experimental import pallas as pl
from jax.experimental.pallas import tpu as pltpu
from jax.sharding import PartitionSpec as P

MESH = pl.DeviceIdType.MESH
F32, BF16 = jnp.float32, jnp.bfloat16
NX, NYH, NZ = 4, 4, 12
ROWS, WIDTH, DEPTH, COLS = 256, 384, 32, 512
K = 3072
OFFSETS = (0, NYH - 1, 1, 2)
def kernel(
    raw, integ, occ_e, occ_p, vir_e, vir_p, order, out,
    amps, ints, pick, parts, moved, vir_sum, occ_sum, turned, place,
    rz, rg, ry, rs, ra, rb, rf, sg, sz, sy, ss, sa, sf, local,
):
    row, col = lax.axis_index("row"), lax.axis_index("col")
    core, z, yh = row % 2, (row // 2) % NZ, row // (2 * NZ)
    x, yl = col % NX, col // NX

    def device(x, yl, yh, z, core):
        return ((yh * NZ + z) * 2 + core, yl * NX + x)

    up, down = device(x, yl, yh, (z + 1) % NZ, core), device(x, yl, yh, (z + NZ - 1) % NZ, core)
    north, south = device(x, yl, (yh + 1) % NYH, z, core), device(x, yl, (yh + NYH - 1) % NYH, z, core)
    east, west = device((x + 1) % NX, yl, yh, z, core), device((x + NX - 1) % NX, yl, yh, z, core)
    up2, down2 = device(x, yl, yh, (z + 2) % NZ, core), device(x, yl, yh, (z + NZ - 2) % NZ, core)
    partner, sibling = device(x, 1 - yl, yh, z, core), device(x, yl, yh, z, 1 - core)
    along_z = (up, down)

    def slot(z, core, yh):
        return z * 8 + core * 4 + yh

    def send(src, dst, ssem, rsem, to):
        pltpu.make_async_remote_copy(
            src_ref=src, dst_ref=dst, send_sem=ssem, recv_sem=rsem, device_id=to, device_id_type=MESH
        ).start()

    def wait(ref, sem):
        pltpu.make_async_copy(ref, ref, sem).wait()

    barrier = pltpu.get_barrier_semaphore()
    for to in (up, down, up2, down2, north, south, east, west, partner, sibling):
        pl.semaphore_signal(barrier, inc=1, device_id=to, device_id_type=MESH)
    pl.semaphore_wait(barrier, 10)

    own = slot(z, core, yh)
    mine = ints.at[own]
    for h in range(2):
        for way, to in ((0, north), (1, south)):
            g = (h, 1 - h)[way]
            send(integ.at[pl.ds(g * 16, 16)], ints.at[own, pl.ds(g * 16, 16)], sy.at[way], ry.at[way, g], to)
    send(integ, mine, sz.at[0], rz.at[0, 0, 0], up)
    send(integ, mine, sz.at[1], rz.at[1, 0, 0], down)
    send(integ, mine, sz.at[0], rz.at[0, 1, 0], up2)
    send(integ, mine, sz.at[1], rz.at[1, 1, 0], down2)
    g0, g1 = yl * NX, (1 - yl) * NX
    x_w, x_e, x_o = (x + NX - 1) % NX, (x + 1) % NX, (x + 2) % NX

    def half(block, h):
        return amps.at[block, pl.ds(h * (ROWS // 2), ROWS // 2)]

    for h in range(2):
        for way, to in ((0, east), (1, west)):
            send(raw.at[pl.ds(h * (ROWS // 2), ROWS // 2)], half(col, h), sa.at[way], ra.at[way, h], to)
    keep_b = pltpu.make_async_copy(integ, mine, local.at[0])
    keep_a = pltpu.make_async_copy(raw, amps.at[col], local.at[1])
    keep_b.start()
    keep_a.start()

    sub = lax.broadcasted_iota(jnp.int32, (ROWS, 256), 0)
    lane = lax.broadcasted_iota(jnp.int32, (ROWS, 256), 1)
    energy = jnp.broadcast_to(occ_e[...], (ROWS, 256))
    total = jnp.zeros((ROWS, 1), F32)
    for j in range(2):
        orbital = jnp.broadcast_to(occ_p[j : j + 1, :].astype(F32), (ROWS, 256))
        orbital = jnp.sum(jnp.where(sub == lane, orbital, 0.0), axis=1, keepdims=True)
        total += jnp.sum(jnp.where(lane.astype(F32) == orbital, energy, 0.0), axis=1, keepdims=True)
    occ_sum[...] = total

    for shift in range(4):
        turned[shift] = order[...] if shift == 0 else pltpu.roll(order[...], shift * 32, 1)
    quarter = lax.broadcasted_iota(jnp.int32, (1, 128), 1) // 32
    for zs in range(NZ):
        for c in range(2):
            found = None
            for ys in range(NYH):
                here = turned[(ys - zs % 2 * 2 - c) % 4, pl.ds(ys * 6 + zs // 2, 1), :]
                found = here if found is None else jnp.where(quarter == ys, here, found)
            place[:, pl.ds(zs * 256 + c * 128, 128)] = found

    table = vir_e[...]
    hi = table.astype(BF16)
    rest = table - hi.astype(F32)
    mid = rest.astype(BF16)
    low = (rest - mid.astype(F32)).astype(BF16)
    table = jnp.concatenate([hi, mid, low], axis=0)

    def vir_block(b, carry):
        total = jnp.zeros((1, WIDTH), F32)
        for j in range(2):
            index = vir_p[pl.ds(j, 1), pl.ds(pl.multiple_of(b * WIDTH, 128), WIDTH)]
            major = index // 128
            minor = index - major * 128
            hot = jnp.where(lax.broadcasted_iota(jnp.int32, (128, WIDTH), 0) == minor, 1.0, 0.0).astype(BF16)
            found = jnp.dot(table, hot, preferred_element_type=F32)
            found = found[0:16] + found[16:32] + found[32:48]
            total += jnp.sum(
                jnp.where(lax.broadcasted_iota(jnp.int32, (16, WIDTH), 0) == major, found, 0.0), axis=0, keepdims=True
            )
        vir_sum[b] = total
        return carry

    blocks = [col, g0 + x_w, g0 + x_e, g1 + x, g0 + x_o, g1 + x_e, g1 + x_w, g1 + x_o]

    def fill(p):
        def some(i, carry):
            hot = lax.broadcasted_iota(jnp.int32, (64, K), 0) + (blocks[p] * WIDTH + i * 64) == place[...]
            pick[pl.ds(pl.multiple_of(p * WIDTH + i * 64, 64), 64), :] = jnp.where(hot, 1.0, 0.0).astype(BF16)
            return carry

        lax.fori_loop(0, 6, some, 0)

    def scale(p):
        scaled = amps[blocks[p]] / (vir_sum[blocks[p]] - occ_sum[...])
        hi = scaled.astype(BF16)
        parts[0:ROWS, p * WIDTH : (p + 1) * WIDTH] = hi
        parts[ROWS:, p * WIDTH : (p + 1) * WIDTH] = (scaled - hi.astype(F32)).astype(BF16)

    def permute(p, count, events=()):
        def some(i, carry):
            at = pl.ds(pl.multiple_of(i * 1024, 1024), 1024)
            here = slice(p * WIDTH, (p + count) * WIDTH)
            new = jnp.dot(parts[:, here], pick[here, at], preferred_element_type=F32).astype(BF16)
            moved[:, at] = new if p == 0 else moved[:, at] + new
            for j, event in enumerate(events):
                pl.when(i == j)(event)
            return carry

        lax.fori_loop(0, 3, some, 0)

    def contract(chosen):
        rows = jnp.concatenate(
            [ints[pl.ds(z_from * 8 + first, n)].reshape(n * DEPTH, COLS) for z_from, first, n in chosen], axis=0
        )
        hi = rows.astype(BF16)
        low = (rows - hi.astype(F32)).astype(BF16)
        at = [
            pl.ds(pl.multiple_of(z_from * 256 + first * DEPTH, 128), n * DEPTH) for z_from, first, n in chosen
        ]
        a_hi = jnp.concatenate([moved[0:ROWS, cols] for cols in at], axis=1)
        a_low = jnp.concatenate([moved[ROWS:, cols] for cols in at], axis=1)
        out[...] += (
            jnp.dot(a_hi, hi, preferred_element_type=F32)
            + jnp.dot(a_low, hi, preferred_element_type=F32)
            + jnp.dot(a_hi, low, preferred_element_type=F32)
        )

    y_slots = [slot(z, core, (yh + off) % NYH) for off in OFFSETS]

    def plane(u, h):
        here = piece(y_slots[u], h)
        for way in range(2):
            send(here, here, sz.at[way], rz.at[way, 0, u], along_z[way])

    def piece(s, h):
        return ints.at[s, pl.ds(h * 16, 16)]

    def group(z, core):
        return ints.at[pl.ds(slot(z, core, 0), 4)]

    def to_sibling(z_from, index):
        send(group(z_from, core), group(z_from, core), ss, rs.at[index], sibling)

    def source(t, way):
        return (z + (NZ - t, t)[way]) % NZ

    def block_to_sibling(s, index):
        send(ints.at[s], ints.at[s], ss, rs.at[index], sibling)

    def eighth(way, u, h):
        return ints.at[slot(source(3, way), core, (yh + OFFSETS[u]) % NYH), pl.ds(h * 8, 8)]

    def mid_on():
        for way in range(2):
            for side, to in ((0, north), (1, south)):
                wait(piece(slot(source(3, way), core, (yh + OFFSETS[1 + side]) % NYH), 0), rg.at[way, side])
                here = eighth(way, 1 + side, side)
                send(here, here, sg.at[way, side], rg.at[way, 2 + side], to)

    def hop(t, u):
        for way in range(2):
            s = slot(source(t, way), core, (yh + OFFSETS[u]) % NYH)
            wait(piece(s, 1) if t == 3 and u else ints.at[s], rz.at[way, t - 1, u])
            if t == 3 and u == 0:
                for side, to in ((0, north), (1, south)):
                    send(piece(s, 0), piece(s, 0), sg.at[way, side], rg.at[way, side], to)
            if t == 3 and u == 3:
                for side in range(2):
                    wait(eighth(way, 3, side), rg.at[way, 2 + side])
            if t < 5 and (t, u) != (1, 0):
                here = piece(s, 1) if t == 2 and u else ints.at[s]
                send(here, here, sz.at[way], rz.at[way, t, u], along_z[way])
            elif t == 5 and u == 0:
                send(piece(s, way), piece(s, way), sz.at[way], rz.at[way, 5, 0], along_z[way])
            if t == 5:
                block_to_sibling(s, 9 + way)
            elif u == 3:
                to_sibling(source(t, way), 2 * t - 1 + way)

    def quarter_of(block, h, way):
        return amps.at[block, pl.ds(h * (ROWS // 2) + way * (ROWS // 4), ROWS // 4)]

    def amps_in(far, h):
        for way, p in ((0, (1, 6)[far]), (1, (2, 5)[far])):
            wait(half(blocks[p], h), ra.at[(0, 3)[far] + way, h])
            here = quarter_of(blocks[p], h, way)
            send(here, here, sa.at[way], rb.at[far, h, way], (east, west)[way])

    def partner_in(h):
        wait(half(blocks[3], h), ra.at[2, h])
        for way in range(2):
            here = half(blocks[3], h)
            send(here, here, sa.at[way], ra.at[3 + way, h], (east, west)[way])

    def opposite_in(far):
        for h in range(2):
            for way in range(2):
                wait(quarter_of(blocks[(4, 7)[far]], h, way), rb.at[far, h, way])

    z_far = (z + 6) % NZ
    f_slots = [slot(z_far, core, (yh + off) % NYH) for off in OFFSETS]

    def far_in():
        for way in range(2):
            here = piece(f_slots[0], way)
            wait(here, rz.at[way, 5, 0])
            send(here, here, sf.at[0], rf.at[0, way], north)
            send(here, here, sf.at[1], rf.at[1, way], south)

    def far_on():
        for way in range(2):
            here = piece(f_slots[1 + way], way)
            wait(here, rf.at[way, way])
            send(here, here, sf.at[way], rf.at[2, way], (north, south)[way])

    def far_end():
        for way in range(2):
            wait(piece(f_slots[1 + way], 1 - way), rf.at[way, 1 - way])
            wait(piece(f_slots[3], way), rf.at[2, way])
        to_sibling(z_far, 11)

    def side_in(h, way):
        wait(piece(y_slots[1 + way], h), ry.at[way, h])
        if h == way:
            send(piece(y_slots[1 + way], h), piece(y_slots[1 + way], h), sy.at[2 + way], ry.at[2, way], (north, south)[way])
        plane(1 + way, h)

    def steps(*calls):
        def event():
            for call, *args in calls:
                call(*args)

        return event

    def plane_end():
        for h in range(2):
            wait(piece(y_slots[3], h), ry.at[2, h])
            plane(3, h)
        keep_b.wait()
        to_sibling(z, 0)

    lax.fori_loop(0, 8, vir_block, 0)
    fill(0)
    fill(1)
    keep_a.wait()
    scale(0)
    side_in(0, 0)
    side_in(1, 1)
    for h in range(2):
        send(raw.at[pl.ds(h * (ROWS // 2), ROWS // 2)], half(col, h), sa.at[2], ra.at[2, h], partner)
    fill(2)
    side_in(1, 0)
    side_in(0, 1)
    hop(1, 0)
    hop(2, 0)
    permute(0, 1, [steps((amps_in, 0, 0)), steps((plane_end,))])
    fill(3)
    hop(1, 1)
    fill(4)
    amps_in(0, 1)
    hop(3, 0)
    scale(1)
    scale(2)
    hop(1, 2)
    hop(1, 3)
    partner_in(0)
    permute(1, 2, [steps((hop, 2, 1)), steps((hop, 4, 0)), steps((hop, 2, 2))])
    partner_in(1)
    fill(5)
    hop(2, 3)
    opposite_in(0)
    scale(3)
    scale(4)
    hop(5, 0)
    mid_on()
    hop(3, 1)
    amps_in(1, 0)
    permute(3, 2, [steps((hop, 3, 2)), steps((far_in,), (hop, 3, 3)), steps((amps_in, 1, 1))])
    scale(5)
    scale(6)
    hop(4, 1)
    fill(6)
    fill(7)
    permute(5, 2, [steps((hop, 4, 2)), steps((hop, 4, 3)), steps((far_on,))])
    opposite_in(1)
    scale(7)
    permute(7, 1, [steps((hop, 5, 1)), steps((hop, 5, 2)), steps((hop, 5, 3))])
    for i in range(9):
        wait(group(z, 0), rs.at[i])
    out[...] = jnp.zeros_like(out)

    def near(i, carry):
        contract([((z + 8 + i * 3 + j) % NZ, 0, 8) for j in range(3)])
        pl.when(i == 0)(far_end)
        return carry

    lax.fori_loop(0, 3, near, 0)
    contract([(z_from, core * 4, 4) for z_from in ((z + 5) % NZ, z_far, (z + 7) % NZ)])
    for i in range(9, 12):
        wait(group(z, 0), rs.at[i])
    contract([(z_from, 4 - core * 4, 4) for z_from in ((z + 5) % NZ, z_far, (z + 7) % NZ)])

    for way in range(2):
        wait(ints.at[pl.ds(0, 19)], sz.at[way])
        for side in range(2):
            wait(ints.at[pl.ds(0, 3), pl.ds(0, 8)], sg.at[way, side])
        wait(ints.at[0], sy.at[way])
        wait(piece(0, 0), sy.at[2 + way])
        wait(ints.at[pl.ds(0, 3), pl.ds(0, 16)], sf.at[way])
        wait(amps.at[pl.ds(0, 3)], sa.at[way])
    wait(amps.at[0], sa.at[2])
    wait(ints.at[pl.ds(0, 48)], ss)


def on_device(raw_amps, integrals, occ_energy, vir_energy, occ_pairs, vir_pairs, pair_order):
    vmem = pl.BlockSpec(memory_space=pltpu.VMEM)
    hbm = pl.BlockSpec(memory_space=pl.ANY)
    dma = pltpu.SemaphoreType.DMA
    return pl.pallas_call(
        kernel,
        out_shape=pltpu.VMEM((ROWS, COLS), F32),
        in_specs=[hbm, hbm] + [vmem] * 5,
        out_specs=vmem,
        scratch_shapes=[
            pltpu.VMEM((8, ROWS, WIDTH), F32),
            pltpu.VMEM((96, DEPTH, COLS), F32),
            pltpu.VMEM((K, K), BF16),
            pltpu.VMEM((2 * ROWS, K), BF16),
            pltpu.VMEM((2 * ROWS, K), BF16),
            pltpu.VMEM((8, 1, WIDTH), F32),
            pltpu.VMEM((ROWS, 1), F32),
            pltpu.VMEM((4, 24, 128), jnp.int32),
            pltpu.VMEM((1, K), jnp.int32),
            dma((2, 6, 4)),
            dma((2, 4)),
            dma((3, 2)),
            dma((12,)),
            dma((5, 2)),
            dma((2, 2, 2)),
            dma((3, 2)),
            dma((2, 2)),
            dma((2,)),
            dma((4,)),
            dma(()),
            dma((3,)),
            dma((2,)),
            dma((2,)),
        ],
        compiler_params=pltpu.CompilerParams(
            collective_id=0, has_side_effects=True, vmem_limit_bytes=56 << 20
        ),
    )(
        raw_amps,
        integrals,
        occ_energy.reshape(1, 256),
        occ_pairs.T,
        vir_energy.reshape(16, 128),
        vir_pairs.T,
        pair_order.reshape(24, 128),
    )


def solution(mesh):
    placed = (P("row", "col"), P("row", "col"), P(), P(), P("row", None), P(), P())
    return jax.shard_map(
        on_device, mesh=mesh, in_specs=placed, out_specs=P("row", "col"), check_vma=False
    )
```

```python
import functools

import jax
import jax.numpy as jnp
from jax import lax
from jax.experimental import pallas as pl
from jax.experimental.pallas import tpu as pltpu
from jax.sharding import PartitionSpec as P

MESH = pl.DeviceIdType.MESH
F32, BF16 = jnp.float32, jnp.bfloat16
NX, NYH, NZ = 4, 4, 12
ROWS, WIDTH, DEPTH, COLS = 256, 384, 32, 512
K = 3072
OFFSETS = (0, NYH - 1, 1, 2)
def kernel(
    raw, integ, occ_e, occ_p, vir_e, vir_p, order, out,
    amps, ints, pick, parts, moved, vir_sum, occ_sum, turned, place,
    rz, rg, ry, rs, ra, rb, rf, sg, sz, sy, ss, sa, sf, local,
):
    row, col = lax.axis_index("row"), lax.axis_index("col")
    core, z, yh = row % 2, (row // 2) % NZ, row // (2 * NZ)
    x, yl = col % NX, col // NX

    def device(x, yl, yh, z, core):
        return ((yh * NZ + z) * 2 + core, yl * NX + x)

    up, down = device(x, yl, yh, (z + 1) % NZ, core), device(x, yl, yh, (z + NZ - 1) % NZ, core)
    north, south = device(x, yl, (yh + 1) % NYH, z, core), device(x, yl, (yh + NYH - 1) % NYH, z, core)
    east, west = device((x + 1) % NX, yl, yh, z, core), device((x + NX - 1) % NX, yl, yh, z, core)
    up2, down2 = device(x, yl, yh, (z + 2) % NZ, core), device(x, yl, yh, (z + NZ - 2) % NZ, core)
    partner, sibling = device(x, 1 - yl, yh, z, core), device(x, yl, yh, z, 1 - core)
    along_z = (up, down)

    def slot(z, core, yh):
        return z * 8 + core * 4 + yh

    def send(src, dst, ssem, rsem, to):
        pltpu.make_async_remote_copy(
            src_ref=src, dst_ref=dst, send_sem=ssem, recv_sem=rsem, device_id=to, device_id_type=MESH
        ).start()

    def wait(ref, sem):
        pltpu.make_async_copy(ref, ref, sem).wait()

    barrier = pltpu.get_barrier_semaphore()
    for to in (up, down, up2, down2, north, south, east, west, partner, sibling):
        pl.semaphore_signal(barrier, inc=1, device_id=to, device_id_type=MESH)
    pl.semaphore_wait(barrier, 10)

    own = slot(z, core, yh)
    mine = ints.at[own]
    for h in range(2):
        for way, to in ((0, north), (1, south)):
            g = (h, 1 - h)[way]
            send(integ.at[pl.ds(g * 16, 16)], ints.at[own, pl.ds(g * 16, 16)], sy.at[way], ry.at[way, g], to)
    send(integ, mine, sz.at[0], rz.at[0, 0, 0], up)
    send(integ, mine, sz.at[1], rz.at[1, 0, 0], down)
    send(integ, mine, sz.at[0], rz.at[0, 1, 0], up2)
    send(integ, mine, sz.at[1], rz.at[1, 1, 0], down2)
    g0, g1 = yl * NX, (1 - yl) * NX
    x_w, x_e, x_o = (x + NX - 1) % NX, (x + 1) % NX, (x + 2) % NX

    def half(block, h):
        return amps.at[block, pl.ds(h * (ROWS // 2), ROWS // 2)]

    for h in range(2):
        for way, to in ((0, east), (1, west)):
            send(raw.at[pl.ds(h * (ROWS // 2), ROWS // 2)], half(col, h), sa.at[way], ra.at[way, h], to)
    keep_b = pltpu.make_async_copy(integ, mine, local.at[0])
    keep_a = pltpu.make_async_copy(raw, amps.at[col], local.at[1])
    keep_b.start()
    keep_a.start()

    sub = lax.broadcasted_iota(jnp.int32, (ROWS, 256), 0)
    lane = lax.broadcasted_iota(jnp.int32, (ROWS, 256), 1)
    energy = jnp.broadcast_to(occ_e[...], (ROWS, 256))
    total = jnp.zeros((ROWS, 1), F32)
    for j in range(2):
        orbital = jnp.broadcast_to(occ_p[j : j + 1, :].astype(F32), (ROWS, 256))
        orbital = jnp.sum(jnp.where(sub == lane, orbital, 0.0), axis=1, keepdims=True)
        total += jnp.sum(jnp.where(lane.astype(F32) == orbital, energy, 0.0), axis=1, keepdims=True)
    occ_sum[...] = total

    for shift in range(4):
        turned[shift] = order[...] if shift == 0 else pltpu.roll(order[...], shift * 32, 1)
    quarter = lax.broadcasted_iota(jnp.int32, (1, 128), 1) // 32
    for zs in range(NZ):
        for c in range(2):
            found = None
            for ys in range(NYH):
                here = turned[(ys - zs % 2 * 2 - c) % 4, pl.ds(ys * 6 + zs // 2, 1), :]
                found = here if found is None else jnp.where(quarter == ys, here, found)
            place[:, pl.ds(zs * 256 + c * 128, 128)] = found

    table = vir_e[...]
    hi = table.astype(BF16)
    rest = table - hi.astype(F32)
    mid = rest.astype(BF16)
    low = (rest - mid.astype(F32)).astype(BF16)
    table = jnp.concatenate([hi, mid, low], axis=0)

    def vir_block(b, carry):
        total = jnp.zeros((1, WIDTH), F32)
        for j in range(2):
            index = vir_p[pl.ds(j, 1), pl.ds(pl.multiple_of(b * WIDTH, 128), WIDTH)]
            major = index // 128
            minor = index - major * 128
            hot = jnp.where(lax.broadcasted_iota(jnp.int32, (128, WIDTH), 0) == minor, 1.0, 0.0).astype(BF16)
            found = jnp.dot(table, hot, preferred_element_type=F32)
            found = found[0:16] + found[16:32] + found[32:48]
            total += jnp.sum(
                jnp.where(lax.broadcasted_iota(jnp.int32, (16, WIDTH), 0) == major, found, 0.0), axis=0, keepdims=True
            )
        vir_sum[b] = total
        return carry

    blocks = [col, g0 + x_w, g0 + x_e, g1 + x, g0 + x_o, g1 + x_e, g1 + x_w, g1 + x_o]

    def fill(p):
        def some(i, carry):
            hot = lax.broadcasted_iota(jnp.int32, (64, K), 0) + (blocks[p] * WIDTH + i * 64) == place[...]
            pick[pl.ds(pl.multiple_of(p * WIDTH + i * 64, 64), 64), :] = jnp.where(hot, 1.0, 0.0).astype(BF16)
            return carry

        lax.fori_loop(0, 6, some, 0)

    def scale(p):
        scaled = amps[blocks[p]] / (vir_sum[blocks[p]] - occ_sum[...])
        hi = scaled.astype(BF16)
        parts[0:ROWS, p * WIDTH : (p + 1) * WIDTH] = hi
        parts[ROWS:, p * WIDTH : (p + 1) * WIDTH] = (scaled - hi.astype(F32)).astype(BF16)

    def permute(p, count, events=()):
        def some(i, carry):
            at = pl.ds(pl.multiple_of(i * 1024, 1024), 1024)
            here = slice(p * WIDTH, (p + count) * WIDTH)
            new = jnp.dot(parts[:, here], pick[here, at], preferred_element_type=F32).astype(BF16)
            moved[:, at] = new if p == 0 else moved[:, at] + new
            for j, event in enumerate(events):
                pl.when(i == j)(event)
            return carry

        lax.fori_loop(0, 3, some, 0)

    def contract(chosen):
        rows = jnp.concatenate(
            [ints[pl.ds(z_from * 8 + first, n)].reshape(n * DEPTH, COLS) for z_from, first, n in chosen], axis=0
        )
        hi = rows.astype(BF16)
        low = (rows - hi.astype(F32)).astype(BF16)
        at = [
            pl.ds(pl.multiple_of(z_from * 256 + first * DEPTH, 128), n * DEPTH) for z_from, first, n in chosen
        ]
        a_hi = jnp.concatenate([moved[0:ROWS, cols] for cols in at], axis=1)
        a_low = jnp.concatenate([moved[ROWS:, cols] for cols in at], axis=1)
        out[...] += (
            jnp.dot(a_hi, hi, preferred_element_type=F32)
            + jnp.dot(a_low, hi, preferred_element_type=F32)
            + jnp.dot(a_hi, low, preferred_element_type=F32)
        )

    y_slots = [slot(z, core, (yh + off) % NYH) for off in OFFSETS]

    def plane(u, h):
        here = piece(y_slots[u], h)
        for way in range(2):
            send(here, here, sz.at[way], rz.at[way, 0, u], along_z[way])

    def piece(s, h):
        return ints.at[s, pl.ds(h * 16, 16)]

    def group(z, core):
        return ints.at[pl.ds(slot(z, core, 0), 4)]

    def to_sibling(z_from, index):
        send(group(z_from, core), group(z_from, core), ss, rs.at[index], sibling)

    def source(t, way):
        return (z + (NZ - t, t)[way]) % NZ

    def block_to_sibling(s, index):
        send(ints.at[s], ints.at[s], ss, rs.at[index], sibling)

    def eighth(way, u, h):
        return ints.at[slot(source(3, way), core, (yh + OFFSETS[u]) % NYH), pl.ds(h * 8, 8)]

    def mid_on():
        for way in range(2):
            for side, to in ((0, north), (1, south)):
                wait(piece(slot(source(3, way), core, (yh + OFFSETS[1 + side]) % NYH), 0), rg.at[way, side])
                here = eighth(way, 1 + side, side)
                send(here, here, sg.at[way, side], rg.at[way, 2 + side], to)

    def hop(t, u):
        for way in range(2):
            s = slot(source(t, way), core, (yh + OFFSETS[u]) % NYH)
            wait(piece(s, 1) if t == 3 and u else ints.at[s], rz.at[way, t - 1, u])
            if t == 3 and u == 0:
                for side, to in ((0, north), (1, south)):
                    send(piece(s, 0), piece(s, 0), sg.at[way, side], rg.at[way, side], to)
            if t == 3 and u == 3:
                for side in range(2):
                    wait(eighth(way, 3, side), rg.at[way, 2 + side])
            if t < 5 and (t, u) != (1, 0):
                here = piece(s, 1) if t == 2 and u else ints.at[s]
                send(here, here, sz.at[way], rz.at[way, t, u], along_z[way])
            elif t == 5 and u == 0:
                send(piece(s, way), piece(s, way), sz.at[way], rz.at[way, 5, 0], along_z[way])
            if t == 5:
                block_to_sibling(s, 9 + way)
            elif u == 3:
                to_sibling(source(t, way), 2 * t - 1 + way)

    def quarter_of(block, h, way):
        return amps.at[block, pl.ds(h * (ROWS // 2) + way * (ROWS // 4), ROWS // 4)]

    def amps_in(far, h):
        for way, p in ((0, (1, 6)[far]), (1, (2, 5)[far])):
            wait(half(blocks[p], h), ra.at[(0, 3)[far] + way, h])
            here = quarter_of(blocks[p], h, way)
            send(here, here, sa.at[way], rb.at[far, h, way], (east, west)[way])

    def partner_in(h):
        wait(half(blocks[3], h), ra.at[2, h])
        for way in range(2):
            here = half(blocks[3], h)
            send(here, here, sa.at[way], ra.at[3 + way, h], (east, west)[way])

    def opposite_in(far):
        for h in range(2):
            for way in range(2):
                wait(quarter_of(blocks[(4, 7)[far]], h, way), rb.at[far, h, way])

    z_far = (z + 6) % NZ
    f_slots = [slot(z_far, core, (yh + off) % NYH) for off in OFFSETS]

    def far_in():
        for way in range(2):
            here = piece(f_slots[0], way)
            wait(here, rz.at[way, 5, 0])
            send(here, here, sf.at[0], rf.at[0, way], north)
            send(here, here, sf.at[1], rf.at[1, way], south)

    def far_on():
        for way in range(2):
            here = piece(f_slots[1 + way], way)
            wait(here, rf.at[way, way])
            send(here, here, sf.at[way], rf.at[2, way], (north, south)[way])

    def far_end():
        for way in range(2):
            wait(piece(f_slots[1 + way], 1 - way), rf.at[way, 1 - way])
            wait(piece(f_slots[3], way), rf.at[2, way])
        to_sibling(z_far, 11)

    def side_in(h, way):
        wait(piece(y_slots[1 + way], h), ry.at[way, h])
        if h == way:
            send(piece(y_slots[1 + way], h), piece(y_slots[1 + way], h), sy.at[2 + way], ry.at[2, way], (north, south)[way])
        plane(1 + way, h)

    def steps(*calls):
        def event():
            for call, *args in calls:
                call(*args)

        return event

    def plane_end():
        for h in range(2):
            wait(piece(y_slots[3], h), ry.at[2, h])
            plane(3, h)
        keep_b.wait()
        to_sibling(z, 0)

    lax.fori_loop(0, 8, vir_block, 0)
    fill(0)
    fill(1)
    keep_a.wait()
    scale(0)
    side_in(0, 0)
    side_in(1, 1)
    for h in range(2):
        send(raw.at[pl.ds(h * (ROWS // 2), ROWS // 2)], half(col, h), sa.at[2], ra.at[2, h], partner)
    fill(2)
    side_in(1, 0)
    side_in(0, 1)
    hop(1, 0)
    hop(2, 0)
    permute(0, 1, [steps((amps_in, 0, 0)), steps((plane_end,))])
    fill(3)
    hop(1, 1)
    fill(4)
    amps_in(0, 1)
    hop(3, 0)
    scale(1)
    scale(2)
    hop(1, 2)
    hop(1, 3)
    partner_in(0)
    permute(1, 2, [steps((hop, 2, 1)), steps((hop, 4, 0)), steps((hop, 2, 2))])
    partner_in(1)
    fill(5)
    hop(2, 3)
    opposite_in(0)
    scale(3)
    scale(4)
    hop(5, 0)
    mid_on()
    hop(3, 1)
    amps_in(1, 0)
    permute(3, 2, [steps((hop, 3, 2)), steps((far_in,), (hop, 3, 3)), steps((amps_in, 1, 1))])
    scale(5)
    scale(6)
    hop(4, 1)
    fill(6)
    fill(7)
    permute(5, 2, [steps((hop, 4, 2)), steps((hop, 4, 3)), steps((far_on,))])
    opposite_in(1)
    scale(7)
    new = jnp.dot(parts[:, 7 * WIDTH :], pick[7 * WIDTH :, :], preferred_element_type=F32).astype(BF16)
    moved[...] = moved[...] + new
    for u in range(1, 4):
        hop(5, u)
    for i in range(9):
        wait(group(z, 0), rs.at[i])
    out[...] = jnp.zeros_like(out)

    def near(i, carry):
        contract([((z + 8 + i * 3 + j) % NZ, 0, 8) for j in range(3)])
        pl.when(i == 0)(far_end)
        return carry

    lax.fori_loop(0, 3, near, 0)
    contract([(z_from, core * 4, 4) for z_from in ((z + 5) % NZ, z_far, (z + 7) % NZ)])
    for i in range(9, 12):
        wait(group(z, 0), rs.at[i])
    contract([(z_from, 4 - core * 4, 4) for z_from in ((z + 5) % NZ, z_far, (z + 7) % NZ)])

    for way in range(2):
        wait(ints.at[pl.ds(0, 19)], sz.at[way])
        for side in range(2):
            wait(ints.at[pl.ds(0, 3), pl.ds(0, 8)], sg.at[way, side])
        wait(ints.at[0], sy.at[way])
        wait(piece(0, 0), sy.at[2 + way])
        wait(ints.at[pl.ds(0, 3), pl.ds(0, 16)], sf.at[way])
        wait(amps.at[pl.ds(0, 3)], sa.at[way])
    wait(amps.at[0], sa.at[2])
    wait(ints.at[pl.ds(0, 48)], ss)


def on_device(raw_amps, integrals, occ_energy, vir_energy, occ_pairs, vir_pairs, pair_order):
    vmem = pl.BlockSpec(memory_space=pltpu.VMEM)
    hbm = pl.BlockSpec(memory_space=pl.ANY)
    dma = pltpu.SemaphoreType.DMA
    return pl.pallas_call(
        kernel,
        out_shape=pltpu.VMEM((ROWS, COLS), F32),
        in_specs=[hbm, hbm] + [vmem] * 5,
        out_specs=vmem,
        scratch_shapes=[
            pltpu.VMEM((8, ROWS, WIDTH), F32),
            pltpu.VMEM((96, DEPTH, COLS), F32),
            pltpu.VMEM((K, K), BF16),
            pltpu.VMEM((2 * ROWS, K), BF16),
            pltpu.VMEM((2 * ROWS, K), BF16),
            pltpu.VMEM((8, 1, WIDTH), F32),
            pltpu.VMEM((ROWS, 1), F32),
            pltpu.VMEM((4, 24, 128), jnp.int32),
            pltpu.VMEM((1, K), jnp.int32),
            dma((2, 6, 4)),
            dma((2, 4)),
            dma((3, 2)),
            dma((12,)),
            dma((5, 2)),
            dma((2, 2, 2)),
            dma((3, 2)),
            dma((2, 2)),
            dma((2,)),
            dma((4,)),
            dma(()),
            dma((3,)),
            dma((2,)),
            dma((2,)),
        ],
        compiler_params=pltpu.CompilerParams(
            collective_id=0, has_side_effects=True, vmem_limit_bytes=56 << 20
        ),
    )(
        raw_amps,
        integrals,
        occ_energy.reshape(1, 256),
        occ_pairs.T,
        vir_energy.reshape(16, 128),
        vir_pairs.T,
        pair_order.reshape(24, 128),
    )


def solution(mesh):
    placed = (P("row", "col"), P("row", "col"), P(), P(), P("row", None), P(), P())
    return jax.shard_map(
        on_device, mesh=mesh, in_specs=placed, out_specs=P("row", "col"), check_vma=False
    )
```
